512 devices in a mesh: ctx: 32 (over z, core), rep: 16 (over y, x).
Axes of the slice: x: 4, y: 4, z: 16, core: 2. Of those that a mesh axis runs over, the one named last changes fastest.
Arguments:
- queries: bfloat16 [512, 8192], P(None, 'ctx'), may hold values from -6 to 6
- keys: bfloat16 [65536, 1024], P(('ctx', 'rep')), may hold values from -6 to 6
- values: bfloat16 [65536, 1024], P(('ctx', 'rep')), may hold values from -6 to 6
- forward_output: bfloat16 [512, 8192], P(None, 'ctx'), may hold values from -6 to 6
- output_gradient: bfloat16 [512, 8192], P(None, 'ctx'), may hold values from -6 to 6
- log_sum_norm: float32 [64, 512], P('ctx'), may hold values from 3 to 5
- block_attend_mask: int32 [64, 4, 512], P('ctx'), may hold values from 0 to 1, as said below
Outputs:
- grad_queries: bfloat16 [512, 8192], P('rep', 'ctx')
- key_gradient: bfloat16 [65536, 1024], P(('ctx', 'rep'))
- value_gradient: bfloat16 [65536, 1024], P(('ctx', 'rep'))
The draws below stay inside these ranges and needn't reach their ends.
Inputs may be any that keep to these rules, and one draw needn't show every extreme that they name: `block_attend_mask`: 1 where a query block of a query head attends a key block of 128 tokens, else 0; how many key blocks are attended differs from head to head.
All inputs are finite; a program needn't handle non-finite values.
Results may differ from the reference program's by a relative error of at most 0.007.
Values may be sent and summed in bfloat16 or wider, within the bound.
No kernel may reach another device: no remote copies, remote signals or barrier semaphores. Data moves between devices by JAX's collectives and lax.ppermute only.
A program may use at most 64 MiB of HBM per device.

```python
import jax
import jax.numpy as jnp
from jax import lax

QUERY_HEADS = 64
KEY_VALUE_HEADS = 8
HEAD_SIZE = 128
BLK = 128
SLAB_QUERIES = 512
CONTEXT_TOKENS = 65536
QBLK = 4
KBLK = 512
N_CTX = 32


def draw_block_attend_mask(key, part):
    level_key, stripe_key, extra_key = jax.random.split(key, 3)
    levels = jax.random.randint(level_key, (QUERY_HEADS, 1, 1), 2, 9)
    stripes = (jax.random.randint(stripe_key, (QUERY_HEADS, 1, KBLK), 0, 32) < levels).astype(jnp.int32)
    extras = (jax.random.randint(extra_key, (QUERY_HEADS, QBLK, KBLK), 0, 32) < 1).astype(jnp.int32)
    return jnp.maximum(stripes, extras).astype(jnp.int32)


def shard_levels(own_key, shape, cuts, least, largest):
    factor_of, own = 1.0, jax.random.fold_in(own_key, 6)
    for axis_at, shards_of in cuts:
        steps = jnp.exp(jax.random.uniform(jax.random.fold_in(own, axis_at), (shards_of,), jnp.float32, least / len(cuts), largest / len(cuts)))
        factor_of = factor_of * jnp.repeat(steps, shape[axis_at] // shards_of).reshape([-1 if axis == axis_at else 1 for axis in range(len(shape))])
    return factor_of


def gaussian(key, extent, width, most, pieces=(), kind=jnp.bfloat16):
    array = width * jax.random.normal(key, extent, jnp.float32)
    if pieces:
        array = array * shard_levels(key, extent, pieces, -0.22, 0.18)
    return jnp.clip(array, -most, most).astype(kind)


def setup_inputs(seed: int = 0) -> dict:
    arg_keys = jax.random.split(jax.random.key(seed), 8)
    return {
        "queries": gaussian(arg_keys[0], (SLAB_QUERIES, QUERY_HEADS * HEAD_SIZE), 1.0, 6.0, ((1, 32),)),
        "keys": gaussian(arg_keys[1], (CONTEXT_TOKENS, KEY_VALUE_HEADS * HEAD_SIZE), 1.0, 6.0, ((0, 512),)),
        "values": gaussian(arg_keys[2], (CONTEXT_TOKENS, KEY_VALUE_HEADS * HEAD_SIZE), 1.0, 6.0, ((0, 512),)),
        "forward_output": gaussian(arg_keys[3], (SLAB_QUERIES, QUERY_HEADS * HEAD_SIZE), 1.0, 6.0, ((1, 32),)),
        "output_gradient": gaussian(arg_keys[4], (SLAB_QUERIES, QUERY_HEADS * HEAD_SIZE), 1.0, 6.0, ((1, 32),)),
        "log_sum_norm": jnp.clip(3.0 + 2.0 * jax.random.uniform(arg_keys[5], (QUERY_HEADS, SLAB_QUERIES), jnp.float32) ** shard_levels(arg_keys[5], (QUERY_HEADS, SLAB_QUERIES), ((0, 32),), -0.2, 0.2), 3.0, 5.0),
        "block_attend_mask": draw_block_attend_mask(jax.random.fold_in(arg_keys[7], 71), 0),
    }


def round_bf16(value):
    rounded = value.astype(jnp.bfloat16)
    return lax.optimization_barrier(rounded).astype(jnp.float32)


def pair_tree(parts):
    current = list(parts)
    level_count = len(current).bit_length() - 1
    for level in range(level_count):
        current = [round_bf16(current[index] + current[index + 1]) for index in range(0, len(current), 2)]
    return current[0]


def reference(queries, keys, values, forward_output, output_gradient, log_sum_norm, block_attend_mask):
    softmax_scale = HEAD_SIZE ** -0.5
    heads_dev = QUERY_HEADS // N_CTX
    group_members = QUERY_HEADS // KEY_VALUE_HEADS
    key_length = keys.shape[0]
    query_block_count = SLAB_QUERIES // BLK
    key_block_count = key_length // BLK
    highest = lax.Precision.HIGHEST
    full_queries = queries.reshape(SLAB_QUERIES, KEY_VALUE_HEADS, group_members, HEAD_SIZE).transpose(1, 2, 0, 3)
    full_output = forward_output.reshape(SLAB_QUERIES, KEY_VALUE_HEADS, group_members, HEAD_SIZE).transpose(1, 2, 0, 3)
    output_cotangent_full = output_gradient.reshape(SLAB_QUERIES, KEY_VALUE_HEADS, group_members, HEAD_SIZE).transpose(1, 2, 0, 3)
    full_keys = keys.reshape(key_length, KEY_VALUE_HEADS, HEAD_SIZE).transpose(1, 0, 2)
    full_values = values.reshape(key_length, KEY_VALUE_HEADS, HEAD_SIZE).transpose(1, 0, 2)
    full_norm = log_sum_norm.reshape(KEY_VALUE_HEADS, group_members, SLAB_QUERIES)
    full_mask = block_attend_mask.reshape(KEY_VALUE_HEADS, group_members, query_block_count, key_block_count)

    def one_group(items):
        query_g, output_g, cotan_g, key_g, value_g, norm_g, mask_g = items
        key_f32 = key_g.astype(jnp.float32)
        value_f32 = value_g.astype(jnp.float32)
        key_sets = []
        value_sets = []
        key_part = jnp.zeros((key_length, HEAD_SIZE), jnp.float32)
        value_part = jnp.zeros((key_length, HEAD_SIZE), jnp.float32)
        query_grads = []
        for head_index in range(group_members):
            query_h = query_g[head_index].astype(jnp.float32)
            output_h = output_g[head_index].astype(jnp.float32)
            cotan_h = cotan_g[head_index].astype(jnp.float32)
            mask_full = jnp.broadcast_to(mask_g[head_index][:, None, :, None].astype(jnp.float32), (query_block_count, BLK, key_block_count, BLK)).reshape(SLAB_QUERIES, key_length)
            row_dots = jnp.sum(cotan_h * output_h, axis=1)
            scores = jnp.dot(query_h, key_f32.T, precision=highest) * softmax_scale
            weights = jnp.exp(scores - norm_g[head_index][:, None]) * mask_full
            weights_b = round_bf16(weights)
            grad_weights = jnp.dot(cotan_h, value_f32.T, precision=highest)
            grad_scores = round_bf16(weights * (grad_weights - row_dots[:, None]))
            value_part = value_part + jnp.dot(weights_b.T, cotan_h, precision=highest)
            key_part = key_part + jnp.dot(grad_scores.T, query_h, precision=highest)
            query_grads.append((jnp.dot(grad_scores, key_f32, precision=highest) * softmax_scale).astype(jnp.bfloat16))
            if (head_index + 1) % heads_dev == 0:
                key_sets.append(round_bf16(key_part * softmax_scale))
                value_sets.append(round_bf16(value_part))
                key_part = jnp.zeros((key_length, HEAD_SIZE), jnp.float32)
                value_part = jnp.zeros((key_length, HEAD_SIZE), jnp.float32)
        key_total = pair_tree(key_sets)
        value_total = pair_tree(value_sets)
        return key_total.astype(jnp.bfloat16), value_total.astype(jnp.bfloat16), jnp.stack(query_grads)

    key_gradient_parts, value_gradient_parts, query_grads = lax.map(one_group, (full_queries, full_output, output_cotangent_full, full_keys, full_values, full_norm, full_mask))
    grad_queries = query_grads.reshape(QUERY_HEADS, SLAB_QUERIES, HEAD_SIZE).transpose(1, 0, 2).reshape(SLAB_QUERIES, QUERY_HEADS * HEAD_SIZE)
    key_gradient = key_gradient_parts.transpose(1, 0, 2).reshape(key_length, KEY_VALUE_HEADS * HEAD_SIZE)
    value_gradient = value_gradient_parts.transpose(1, 0, 2).reshape(key_length, KEY_VALUE_HEADS * HEAD_SIZE)
    return (grad_queries, key_gradient, value_gradient)
```

```python
import math

import jax
import jax.numpy as jnp
from jax import lax
from jax.experimental import pallas as pl
from jax.experimental.pallas import tpu as pltpu
from jax.sharding import Mesh, PartitionSpec as P


KEY_VALUE_HEADS = 8
HEAD_SIZE = 128
BLK = 128
SLAB_QUERIES = 512
Z, CORES, Y, X = 16, 2, 4, 4
SLOTS = 4
HALF = BLK // 2
TILE = SLAB_QUERIES // (Y * X)
PACKED = 2 * SLAB_QUERIES + 32
PICK = 4
LOG2E = math.log2(math.e)
NEVER = -1e30
f32, bf16 = jnp.float32, jnp.bfloat16


def dot(a, b, dims):
    return lax.dot_general(a, b, (dims, ((), ())), preferred_element_type=f32)


def prepare_kernel(rep, queries, keys, values, output, cotangent, norm, mask, kv, packed):
    for g in range(KEY_VALUE_HEADS):
        lanes = slice(g * HEAD_SIZE, (g + 1) * HEAD_SIZE)
        for half in range(2):
            rows = slice(half * HALF, (half + 1) * HALF)
            kv[2 * g + half, 0] = keys[rows, lanes]
            kv[2 * g + half, 1] = values[rows, lanes]
    packed[:SLAB_QUERIES] = queries[...]
    packed[SLAB_QUERIES:2 * SLAB_QUERIES] = cotangent[...]
    rows = []
    for l in range(2):
        lanes = slice(l * HEAD_SIZE, (l + 1) * HEAD_SIZE)
        product = cotangent[:, lanes].astype(f32) * output[:, lanes].astype(f32)
        rows.append(jnp.sum(product.T, axis=0, keepdims=True))
    rows += [norm[l:l + 1] * (-LOG2E) for l in range(2)]
    wide = 2 * HEAD_SIZE
    exact = jnp.concatenate([r[:, i * wide:(i + 1) * wide] for r in rows for i in range(2)], axis=0)
    high = exact.astype(bf16).astype(f32)
    block = lax.broadcasted_iota(jnp.int32, (CORES * Z * Y * X, HEAD_SIZE), 0)
    lane = lax.broadcasted_iota(jnp.int32, (CORES * Z * Y * X, HEAD_SIZE), 1)
    wanted = ((lane % Z) * CORES + lane // Z) * (Y * X) + rep[0]
    pick = jnp.where((block == wanted) & (lane < CORES * Z), 1.0, 0.0).astype(bf16)
    attend = jnp.concatenate([mask[0], mask[1]], axis=0).astype(f32).astype(bf16)
    picked = dot(attend, pick, ((1,), (0,)))
    zeros = jnp.zeros((8, HEAD_SIZE), f32)
    picked = jnp.concatenate([picked, zeros], axis=1)
    aux = jnp.concatenate([high, exact - high, picked, jnp.zeros((8, wide), f32)], axis=0)
    packed[2 * SLAB_QUERIES:] = aux.astype(bf16)


def prepare(rep, *arrays):
    vmem = pl.BlockSpec(memory_space=pltpu.VMEM)
    return pl.pallas_call(
        prepare_kernel,
        out_shape=(
            jax.ShapeDtypeStruct((Z, 2, HALF, HEAD_SIZE), bf16),
            jax.ShapeDtypeStruct((PACKED, 2 * HEAD_SIZE), bf16),
        ),
        in_specs=[pl.BlockSpec(memory_space=pltpu.SMEM)] + [vmem] * 7,
        out_specs=(vmem, vmem),
        compiler_params=pltpu.CompilerParams(vmem_limit_bytes=12 * 2**20),
        name="prepare",
    )(rep, *arrays)


def to_row_kernel(place, keep, got, own, *sent):
    for d, out in enumerate((own, *sent)):
        for y in range(Y):
            at = pl.multiple_of((y * X + lax.rem(place[0] + d, X)) * TILE, TILE)
            for s in range(2):
                total = keep[s, pl.ds(at, TILE), :] + got[s, pl.ds(at, TILE), :].astype(f32)
                out[s, y] = total.astype(out.dtype)


def to_tile_kernel(place, keep, got1, got2, got3, own, *sent):
    for d, out in enumerate((own, *sent)):
        at = lax.rem(place[0] + d, Y)
        for s in range(2):
            total = keep[s, at]
            for got in (got1, got2, got3):
                total = total + got[s, at].astype(f32)
            out[s] = total.astype(out.dtype)


def reduce_step(kernel, place, shape, *arrays):
    vmem = pl.BlockSpec(memory_space=pltpu.VMEM)
    return pl.pallas_call(
        kernel,
        out_shape=(jax.ShapeDtypeStruct(shape, f32),) + (jax.ShapeDtypeStruct(shape, bf16),) * 3,
        in_specs=[pl.BlockSpec(memory_space=pltpu.SMEM)] + [vmem] * len(arrays),
        out_specs=(vmem,) * 4,
        compiler_params=pltpu.CompilerParams(vmem_limit_bytes=8 * 2**20),
    )(place, *arrays)


def around(value, axis, distance):
    return lax.ppermute(value, axis, [(i, (i + distance) % 4) for i in range(4)])


def attention_kernel(mask, kv, x0, x1, x2, x3, dkv, keep, send,
                     order, qs, gs, norm, dots, kbuf, vbuf, dk, dv, dq):
    scale = HEAD_SIZE ** -0.5
    for s, x in enumerate((x0, x1, x2, x3)):
        aux = x[2 * SLAB_QUERIES:].astype(f32)
        aux = aux[:8] + aux[8:16]
        for l in range(2):
            lanes = slice(l * HEAD_SIZE, (l + 1) * HEAD_SIZE)
            qs[2 * s + l] = x[:SLAB_QUERIES, lanes]
            gs[2 * s + l] = x[SLAB_QUERIES:2 * SLAB_QUERIES, lanes]
            dots[2 * s + l] = jnp.concatenate([aux[2 * l:2 * l + 1], aux[2 * l + 1:2 * l + 2]], axis=1)
            norm[2 * s + l] = jnp.concatenate([aux[2 * l + 4:2 * l + 5], aux[2 * l + 5:2 * l + 6]], axis=1)
    dk[...] = jnp.zeros_like(dk)
    dv[...] = jnp.zeros_like(dv)
    dq[...] = jnp.zeros_like(dq)

    def head(h, _):
        live = []
        for b in range(Z):
            any_of = mask[h * 4, b]
            for qb in range(1, 4):
                any_of = any_of | mask[h * 4 + qb, b]
            live.append(jnp.minimum(any_of, 1))
        n = jnp.int32(0)
        for b in range(Z):
            order[n] = b
            n = n + live[b]
        total = n
        for b in range(Z):
            order[n] = b
            n = n + (1 - live[b])

        def turn(t, _):
            picked = [order[t * PICK + j] for j in range(PICK)]
            rows = []
            for j, i in enumerate(picked):
                kbuf[pl.ds(j * HALF, HALF), :] = kv[i, 0]
                vbuf[pl.ds(j * HALF, HALF), :] = kv[i, 1]
                row = jnp.concatenate(
                    [
                        jnp.where(mask[h * 4 + qb, i] > 0, norm[h, :, pl.ds(qb * BLK, BLK)], NEVER)
                        for qb in range(4)
                    ],
                    axis=1,
                )
                rows.append(jnp.broadcast_to(row, (HALF, SLAB_QUERIES)))
            bias = jnp.concatenate(rows, axis=0)
            q, g = qs[h], gs[h]
            scores = dot(kbuf[...], q, ((1,), (1,)))
            w = jnp.exp2(scores * (scale * LOG2E) + bias)
            gw = dot(vbuf[...], g, ((1,), (1,)))
            ds = (w * (gw - dots[h])).astype(bf16)
            dv_part = dot(w.astype(bf16), g, ((1,), (0,)))
            dk_part = dot(ds, q, ((1,), (0,)))
            for j, i in enumerate(picked):
                dv[i] += dv_part[j * HALF:(j + 1) * HALF]
                dk[i] += dk_part[j * HALF:(j + 1) * HALF]
            dq[h] += dot(kbuf[...], ds, ((0,), (0,)))
            return 0

        lax.fori_loop(0, (total + PICK - 1) // PICK, turn, 0)
        return 0

    lax.fori_loop(0, 2 * SLOTS, head, 0)
    dkv[:, 0] = (dk[...] * scale).astype(bf16)
    dkv[:, 1] = dv[...].astype(bf16)
    for s in range(SLOTS):
        for l in range(2):
            lanes = pl.ds(l * HEAD_SIZE, HEAD_SIZE)
            part = (dq[2 * s + l] * scale).T
            if s % 2 == 0:
                keep[s // 2, :, lanes] = part
            else:
                send[s // 2, :, lanes] = part.astype(bf16)


def attention(mask, kv, xs):
    vmem = pl.BlockSpec(memory_space=pltpu.VMEM)
    rows = (SLAB_QUERIES, 2 * HEAD_SIZE)
    return pl.pallas_call(
        attention_kernel,
        out_shape=(
            jax.ShapeDtypeStruct((Z, 2, HALF, HEAD_SIZE), bf16),
            jax.ShapeDtypeStruct((2, *rows), f32),
            jax.ShapeDtypeStruct((2, *rows), bf16),
        ),
        in_specs=[pl.BlockSpec(memory_space=pltpu.SMEM)] + [vmem] * 5,
        out_specs=(vmem, vmem, vmem),
        scratch_shapes=[
            pltpu.SMEM((2 * Z,), jnp.int32),
            pltpu.VMEM((2 * SLOTS, SLAB_QUERIES, HEAD_SIZE), bf16),
            pltpu.VMEM((2 * SLOTS, SLAB_QUERIES, HEAD_SIZE), bf16),
            pltpu.VMEM((2 * SLOTS, 1, SLAB_QUERIES), f32),
            pltpu.VMEM((2 * SLOTS, 1, SLAB_QUERIES), f32),
            pltpu.VMEM((PICK * HALF, HEAD_SIZE), bf16),
            pltpu.VMEM((PICK * HALF, HEAD_SIZE), bf16),
            pltpu.VMEM((Z, HALF, HEAD_SIZE), f32),
            pltpu.VMEM((Z, HALF, HEAD_SIZE), f32),
            pltpu.VMEM((2 * SLOTS, HEAD_SIZE, SLAB_QUERIES), f32),
        ],
        compiler_params=pltpu.CompilerParams(vmem_limit_bytes=20 * 2**20),
        cost_estimate=pl.CostEstimate(
            flops=5 * 2 * 4096 * 1024 * 128 // 3,
            bytes_accessed=6 * 2**20,
            transcendentals=4096 * 1024 // 3,
        ),
        name="attention",
    )(mask, kv, *xs)


def other_core(value):
    return lax.ppermute(value, "core", [(0, 1), (1, 0)])


def other_chip(value):
    return lax.ppermute(value, "z", [(z, z ^ 1) for z in range(Z)])


def compute(queries, keys, values, forward_output, output_gradient, log_sum_norm, block_attend_mask):
    core, y, x = (lax.axis_index(axis) for axis in ("core", "y", "x"))
    own_kv, x0 = prepare(
        jnp.full((1,), y * X + x, jnp.int32), queries, keys, values, forward_output, output_gradient,
        log_sum_norm, block_attend_mask,
    )
    x2 = other_chip(x0)
    kv = lax.all_to_all(own_kv, "z", 0, 0, tiled=True)
    x1 = other_core(x0)
    x3 = other_core(x2)
    slots = (x0, x1, x2, x3)
    at = 2 * SLAB_QUERIES + 16
    mask = jnp.concatenate(
        [lax.dynamic_slice_in_dim(a[at:at + 8], core * Z, Z, 1) for a in slots]
    ).astype(jnp.int32)

    dkv, keep, send = attention(mask, kv, slots)

    got = other_core(send)
    back = lax.all_to_all(dkv, "z", 0, 0, tiled=True)
    own, *sent = reduce_step(to_row_kernel, jnp.full((1,), x, jnp.int32), (2, Y, TILE, 2 * HEAD_SIZE), keep, got)
    gots = [around(a, "x", d + 1) for d, a in enumerate(sent)]
    own, *sent = reduce_step(to_tile_kernel, jnp.full((1,), y, jnp.int32), (2, TILE, 2 * HEAD_SIZE), own, *gots)
    gots = [around(a, "y", d + 1) for d, a in enumerate(sent)]
    total = own + sum(a.astype(f32) for a in gots)
    other = other_chip(total[1].astype(bf16))
    grad_queries = (total[0] + other.astype(f32)).astype(bf16)

    def in_place(array):
        halves = array.reshape(KEY_VALUE_HEADS, 2, HALF, HEAD_SIZE)
        return halves.transpose(1, 2, 0, 3).reshape(BLK, KEY_VALUE_HEADS * HEAD_SIZE)

    return grad_queries, in_place(back[:, 0]), in_place(back[:, 1])


def solution(mesh):
    fine = Mesh(mesh.devices.reshape(Z, CORES, Y, X), ("z", "core", "y", "x"))
    ctx, rep = ("z", "core"), ("y", "x")
    in_specs = (
        P(None, ctx),
        P((*ctx, *rep), None),
        P((*ctx, *rep), None),
        P(None, ctx),
        P(None, ctx),
        P(ctx, None),
        P(ctx, None, None),
    )
    out_specs = (P(rep, ctx), P((*ctx, *rep), None), P((*ctx, *rep), None))
    return jax.shard_map(compute, mesh=fine, in_specs=in_specs, out_specs=out_specs, check_vma=False)
```

```python
import math

import jax
import jax.numpy as jnp
from jax import lax
from jax.experimental import pallas as pl
from jax.experimental.pallas import tpu as pltpu
from jax.sharding import Mesh, PartitionSpec as P


KEY_VALUE_HEADS = 8
HEAD_SIZE = 128
BLK = 128
SLAB_QUERIES = 512
Z, CORES, Y, X = 16, 2, 4, 4
SLOTS = 4
HALF = BLK // 2
TILE = SLAB_QUERIES // (Y * X)
AUX = 32
PACKED = 2 * SLAB_QUERIES + AUX
PICK = 4
LOG2E = math.log2(math.e)
NEVER = -1e30
f32, bf16 = jnp.float32, jnp.bfloat16


def dot(a, b, dims):
    return lax.dot_general(a, b, (dims, ((), ())), preferred_element_type=f32)


def prepare_kernel(rep, queries, keys, values, output, cotangent, norm, mask, kv, packed,
                   out_buf, norm_buf, mask_buf, sems):
    copies = [
        pltpu.make_async_copy(source, target, sems.at[i])
        for i, (source, target) in enumerate(
            (
                (cotangent, packed.at[pl.ds(SLAB_QUERIES, SLAB_QUERIES)]),
                (output, out_buf),
                (mask, mask_buf),
                (norm, norm_buf),
                (queries, packed.at[pl.ds(0, SLAB_QUERIES)]),
            )
        )
    ]
    for i, source in enumerate((keys, values)):
        for g in range(KEY_VALUE_HEADS):
            for half in range(2):
                part = source.at[pl.ds(half * HALF, HALF), pl.ds(g * HEAD_SIZE, HEAD_SIZE)]
                t = 2 * g + half
                copies.append(pltpu.make_async_copy(part, kv.at[t, i], sems.at[5 + 2 * t + i]))
    for copy in copies:
        copy.start()
    block = lax.broadcasted_iota(jnp.int32, (CORES * Z * Y * X, HEAD_SIZE), 0)
    lane = lax.broadcasted_iota(jnp.int32, (CORES * Z * Y * X, HEAD_SIZE), 1)
    wanted = ((lane % Z) * CORES + lane // Z) * (Y * X) + rep[0]
    pick = jnp.where((block == wanted) & (lane < CORES * Z), 1.0, 0.0).astype(bf16)
    for copy in copies[:4]:
        copy.wait()
    rows = []
    for l in range(2):
        lanes = slice(l * HEAD_SIZE, (l + 1) * HEAD_SIZE)
        own = packed[SLAB_QUERIES:2 * SLAB_QUERIES, lanes]
        product = own.astype(f32) * out_buf[:, lanes].astype(f32)
        rows.append(jnp.sum(product.T, axis=0, keepdims=True))
    rows += [norm_buf[l:l + 1] * (-LOG2E) for l in range(2)]
    wide = 2 * HEAD_SIZE
    exact = jnp.concatenate([r[:, i * wide:(i + 1) * wide] for r in rows for i in range(2)], axis=0)
    high = exact.astype(bf16).astype(f32)
    attend = jnp.concatenate([mask_buf[0], mask_buf[1]], axis=0).astype(f32).astype(bf16)
    picked = dot(attend, pick, ((1,), (0,)))
    picked = jnp.concatenate([picked, jnp.zeros((8, HEAD_SIZE), f32)], axis=1)
    aux = jnp.concatenate([high, exact - high, picked, jnp.zeros((AUX - 24, wide), f32)], axis=0)
    packed[2 * SLAB_QUERIES:] = aux.astype(bf16)
    copies[4].wait()
    for copy in copies[5:]:
        copy.wait()


def prepare(rep, *arrays):
    vmem = pl.BlockSpec(memory_space=pltpu.VMEM)
    wide = 2 * HEAD_SIZE
    return pl.pallas_call(
        prepare_kernel,
        out_shape=(
            jax.ShapeDtypeStruct((Z, 2, HALF, HEAD_SIZE), bf16),
            jax.ShapeDtypeStruct((PACKED, wide), bf16),
        ),
        in_specs=[pl.BlockSpec(memory_space=pltpu.SMEM)] + [pl.BlockSpec(memory_space=pltpu.HBM)] * 7,
        out_specs=(vmem, vmem),
        scratch_shapes=[
            pltpu.VMEM((SLAB_QUERIES, wide), bf16),
            pltpu.VMEM((2, SLAB_QUERIES), f32),
            pltpu.VMEM((2, 4, CORES * Z * Y * X), jnp.int32),
            pltpu.SemaphoreType.DMA((5 + 4 * KEY_VALUE_HEADS,)),
        ],
        name="prepare",
    )(rep, *arrays)


def place_kernel(back, key_grad, value_grad):
    for g in range(KEY_VALUE_HEADS):
        for half in range(2):
            at = (slice(half * HALF, (half + 1) * HALF), slice(g * HEAD_SIZE, (g + 1) * HEAD_SIZE))
            key_grad[at] = back[2 * g + half, 0]
            value_grad[at] = back[2 * g + half, 1]


def placed(back):
    vmem = pl.BlockSpec(memory_space=pltpu.VMEM)
    return pl.pallas_call(
        place_kernel,
        out_shape=(jax.ShapeDtypeStruct((BLK, KEY_VALUE_HEADS * HEAD_SIZE), bf16),) * 2,
        in_specs=[vmem],
        out_specs=(vmem, vmem),
        compiler_params=pltpu.CompilerParams(vmem_limit_bytes=8 * 2**20),
        name="place",
    )(back)


def halve_kernel(bit, keep, got, own, sent):
    mine, other = bit[0], 1 - bit[0]
    for i in range(own.shape[0]):
        own[i] = keep[i, mine].astype(f32) + got[i, mine].astype(f32)
        sent[i] = (keep[i, other].astype(f32) + got[i, other].astype(f32)).astype(bf16)


def halve(bit, keep, got):
    count = keep.size // (2 * TILE * 2 * HEAD_SIZE)
    half = (count, TILE, 2 * HEAD_SIZE)
    whole = (count, 2, TILE, 2 * HEAD_SIZE)
    vmem = pl.BlockSpec(memory_space=pltpu.VMEM)
    return pl.pallas_call(
        halve_kernel,
        out_shape=(jax.ShapeDtypeStruct(half, f32), jax.ShapeDtypeStruct(half, bf16)),
        in_specs=[pl.BlockSpec(memory_space=pltpu.SMEM), vmem, vmem],
        out_specs=(vmem, vmem),
        compiler_params=pltpu.CompilerParams(vmem_limit_bytes=8 * 2**20),
        name="halve",
    )(jnp.full((1,), bit, jnp.int32), keep.reshape(whole), got.reshape(whole))


def across(value, axis, distance):
    return lax.ppermute(value, axis, [(i, i ^ distance) for i in range(4)])


def attention_kernel(mask, order, kv, x0, x1, x2, x3, dkv, keep, send,
                     xs, norm, dots, kbuf, vbuf, dk, dv, dq, sems):
    scale = HEAD_SIZE ** -0.5
    copies = [pltpu.make_async_copy(x, xs.at[s], sems.at[s]) for s, x in enumerate((x0, x1, x2, x3))]
    for copy in copies:
        copy.start()
    dk[...] = jnp.zeros_like(dk)
    dv[...] = jnp.zeros_like(dv)
    dq[...] = jnp.zeros_like(dq)

    def head(h, _):
        for s, copy in enumerate(copies):
            @pl.when(h == 2 * s)
            def _():
                copy.wait()
                aux = xs[s, 2 * SLAB_QUERIES:, :].astype(f32)
                aux = aux[:8] + aux[8:16]
                for l in range(2):
                    dots[2 * s + l] = jnp.concatenate([aux[2 * l:2 * l + 1], aux[2 * l + 1:2 * l + 2]], axis=1)
                    norm[2 * s + l] = jnp.concatenate([aux[2 * l + 4:2 * l + 5], aux[2 * l + 5:2 * l + 6]], axis=1)

        s, lanes = h // 2, pl.ds(pl.multiple_of((h % 2) * HEAD_SIZE, HEAD_SIZE), HEAD_SIZE)

        def turn(t, _):
            picked = [order[h, t * PICK + j] for j in range(PICK)]
            rows = []
            for j, i in enumerate(picked):
                kbuf[pl.ds(j * HALF, HALF), :] = kv[i, 0]
                vbuf[pl.ds(j * HALF, HALF), :] = kv[i, 1]
                row = jnp.concatenate(
                    [
                        jnp.where(mask[h * 4 + qb, i] > 0, norm[h, :, pl.ds(qb * BLK, BLK)], NEVER)
                        for qb in range(4)
                    ],
                    axis=1,
                )
                rows.append(jnp.broadcast_to(row, (HALF, SLAB_QUERIES)))
            bias = jnp.concatenate(rows, axis=0)
            q, g = xs[s, :SLAB_QUERIES, lanes], xs[s, SLAB_QUERIES:2 * SLAB_QUERIES, lanes]
            scores = dot(kbuf[...], q, ((1,), (1,)))
            w = jnp.exp2(scores * (scale * LOG2E) + bias)
            gw = dot(vbuf[...], g, ((1,), (1,)))
            ds = (w * (gw - dots[h])).astype(bf16)
            dv_part = dot(w.astype(bf16), g, ((1,), (0,)))
            dk_part = dot(ds, q, ((1,), (0,)))
            for j, i in enumerate(picked):
                dv[i] += dv_part[j * HALF:(j + 1) * HALF]
                dk[i] += dk_part[j * HALF:(j + 1) * HALF]
            dq[h] += dot(kbuf[...], ds, ((0,), (0,)))
            return 0

        lax.fori_loop(0, order[h, Z], turn, 0)
        return 0

    lax.fori_loop(0, 2 * SLOTS, head, 0)
    dkv[:, 0] = (dk[...] * scale).astype(bf16)
    dkv[:, 1] = dv[...].astype(bf16)
    for s in range(SLOTS):
        for l in range(2):
            lanes = pl.ds(l * HEAD_SIZE, HEAD_SIZE)
            part = (dq[2 * s + l] * scale).astype(bf16).T
            if s % 2 == 0:
                keep[s // 2, :, lanes] = part
            else:
                send[s // 2, :, lanes] = part


def attention(mask, order, kv, xs):
    vmem = pl.BlockSpec(memory_space=pltpu.VMEM)
    rows = (SLAB_QUERIES, 2 * HEAD_SIZE)
    return pl.pallas_call(
        attention_kernel,
        out_shape=(
            jax.ShapeDtypeStruct((Z, 2, HALF, HEAD_SIZE), bf16),
            jax.ShapeDtypeStruct((2, *rows), bf16),
            jax.ShapeDtypeStruct((2, *rows), bf16),
        ),
        in_specs=[pl.BlockSpec(memory_space=pltpu.SMEM)] * 2 + [vmem] + [pl.BlockSpec(memory_space=pl.ANY)] * 4,
        out_specs=(vmem, vmem, vmem),
        scratch_shapes=[
            pltpu.VMEM((SLOTS, PACKED, 2 * HEAD_SIZE), bf16),
            pltpu.VMEM((2 * SLOTS, 1, SLAB_QUERIES), f32),
            pltpu.VMEM((2 * SLOTS, 1, SLAB_QUERIES), f32),
            pltpu.VMEM((PICK * HALF, HEAD_SIZE), bf16),
            pltpu.VMEM((PICK * HALF, HEAD_SIZE), bf16),
            pltpu.VMEM((Z, HALF, HEAD_SIZE), f32),
            pltpu.VMEM((Z, HALF, HEAD_SIZE), f32),
            pltpu.VMEM((2 * SLOTS, HEAD_SIZE, SLAB_QUERIES), f32),
            pltpu.SemaphoreType.DMA((SLOTS,)),
        ],
        compiler_params=pltpu.CompilerParams(vmem_limit_bytes=28 * 2**20),
        cost_estimate=pl.CostEstimate(
            flops=5 * 2 * 4096 * 1024 * 128 // 3,
            bytes_accessed=6 * 2**20,
            transcendentals=4096 * 1024 // 3,
        ),
        name="attention",
    )(mask, order, kv, *xs)


def attended_first(mask):
    live = jnp.max(mask.reshape(2 * SLOTS, 4, Z), axis=1)
    index = jnp.arange(Z)
    earlier = (index[:, None] < index[None, :]).astype(jnp.int32)
    before = jnp.sum(live[:, :, None] * earlier, axis=1)
    count = jnp.sum(live, axis=1, keepdims=True)
    rank = jnp.where(live > 0, before, count + index[None, :] - before)
    order = jnp.sum(jnp.where(rank[:, :, None] == index, index[None, :, None], 0), axis=1)
    return jnp.concatenate([order, (count + PICK - 1) // PICK], axis=1).astype(jnp.int32)


def other_core(value):
    return lax.ppermute(value, "core", [(0, 1), (1, 0)])


def other_chip(value):
    return lax.ppermute(value, "z", [(z, z ^ 1) for z in range(Z)])


def compute(queries, keys, values, forward_output, output_gradient, log_sum_norm, block_attend_mask):
    core, y, x = (lax.axis_index(axis) for axis in ("core", "y", "x"))
    own_kv, x0 = prepare(
        jnp.full((1,), y * X + x, jnp.int32), queries, keys, values, forward_output, output_gradient,
        log_sum_norm, block_attend_mask,
    )
    x2 = other_chip(x0)
    kv = lax.all_to_all(own_kv, "z", 0, 0, tiled=True)
    x1 = other_core(x0)
    x3 = other_core(x2)
    slots = (x0, x1, x2, x3)
    at = 2 * SLAB_QUERIES + 16
    attended = [a[at:at + 8] for a in slots[:3]]
    attended.append(other_core(attended[2]))
    mask = jnp.concatenate(
        [lax.dynamic_slice_in_dim(a, core * Z, Z, 1) for a in attended]
    ).astype(jnp.int32)

    dkv, keep, send = attention(mask, attended_first(mask), kv, slots)

    got = other_core(send)
    own, sent = halve(x % 2, keep, got)
    got = across(sent, "x", 1)
    back = lax.all_to_all(dkv, "z", 0, 0, tiled=True)
    for bit, axis, distance in ((x // 2, "x", 2), (y % 2, "y", 1), (y // 2, "y", 2)):
        own, sent = halve(bit, own, got)
        got = across(sent, axis, distance)
    total = own + got.astype(f32)
    other = other_chip(total[1].astype(bf16))
    grad_queries = (total[0] + other.astype(f32)).astype(bf16)
    key_grad, value_grad = placed(back)
    return grad_queries, key_grad, value_grad


def solution(mesh):
    fine = Mesh(mesh.devices.reshape(Z, CORES, Y, X), ("z", "core", "y", "x"))
    ctx, rep = ("z", "core"), ("y", "x")
    in_specs = (
        P(None, ctx),
        P((*ctx, *rep), None),
        P((*ctx, *rep), None),
        P(None, ctx),
        P(None, ctx),
        P(ctx, None),
        P(ctx, None, None),
    )
    out_specs = (P(rep, ctx), P((*ctx, *rep), None), P((*ctx, *rep), None))
    return jax.shard_map(compute, mesh=fine, in_specs=in_specs, out_specs=out_specs, check_vma=False)
```

```python
import math

import jax
import jax.numpy as jnp
from jax import lax
from jax.experimental import pallas as pl
from jax.experimental.pallas import tpu as pltpu
from jax.sharding import Mesh, PartitionSpec as P


KEY_VALUE_HEADS = 8
HEAD_SIZE = 128
BLK = 128
SLAB_QUERIES = 512
Z, CORES, Y, X = 16, 2, 4, 4
SLOTS = 4
HALF = BLK // 2
TILE = SLAB_QUERIES // (Y * X)
AUX = 32
PACKED = 2 * SLAB_QUERIES + AUX
PICK = 4
LOG2E = math.log2(math.e)
NEVER = -1e30
f32, bf16 = jnp.float32, jnp.bfloat16


def dot(a, b, dims):
    return lax.dot_general(a, b, (dims, ((), ())), preferred_element_type=f32)


def prepare_kernel(rep, queries, keys, values, output, cotangent, norm, mask, kv, packed,
                   out_buf, norm_buf, mask_buf, sems):
    copies = [
        pltpu.make_async_copy(source, target, sems.at[i])
        for i, (source, target) in enumerate(
            (
                (cotangent, packed.at[pl.ds(SLAB_QUERIES, SLAB_QUERIES)]),
                (output, out_buf),
                (mask, mask_buf),
                (norm, norm_buf),
                (queries, packed.at[pl.ds(0, SLAB_QUERIES)]),
            )
        )
    ]
    for i, source in enumerate((keys, values)):
        for g in range(KEY_VALUE_HEADS):
            for half in range(2):
                part = source.at[pl.ds(half * HALF, HALF), pl.ds(g * HEAD_SIZE, HEAD_SIZE)]
                t = 2 * g + half
                copies.append(pltpu.make_async_copy(part, kv.at[t, i], sems.at[5 + 2 * t + i]))
    for copy in copies:
        copy.start()
    block = lax.broadcasted_iota(jnp.int32, (CORES * Z * Y * X, HEAD_SIZE), 0)
    lane = lax.broadcasted_iota(jnp.int32, (CORES * Z * Y * X, HEAD_SIZE), 1)
    wanted = ((lane % Z) * CORES + lane // Z) * (Y * X) + rep[0]
    pick = jnp.where((block == wanted) & (lane < CORES * Z), 1.0, 0.0).astype(bf16)
    for copy in copies[:4]:
        copy.wait()
    rows = []
    for l in range(2):
        lanes = slice(l * HEAD_SIZE, (l + 1) * HEAD_SIZE)
        own = packed[SLAB_QUERIES:2 * SLAB_QUERIES, lanes]
        product = own.astype(f32) * out_buf[:, lanes].astype(f32)
        rows.append(jnp.sum(product.T, axis=0, keepdims=True))
    rows += [norm_buf[l:l + 1] * (-LOG2E) for l in range(2)]
    wide = 2 * HEAD_SIZE
    exact = jnp.concatenate([r[:, i * wide:(i + 1) * wide] for r in rows for i in range(2)], axis=0)
    high = exact.astype(bf16).astype(f32)
    attend = jnp.concatenate([mask_buf[0], mask_buf[1]], axis=0).astype(f32).astype(bf16)
    picked = dot(attend, pick, ((1,), (0,)))
    picked = jnp.concatenate([picked, jnp.zeros((8, HEAD_SIZE), f32)], axis=1)
    aux = jnp.concatenate([high, exact - high, picked, jnp.zeros((AUX - 24, wide), f32)], axis=0)
    packed[2 * SLAB_QUERIES:] = aux.astype(bf16)
    copies[4].wait()
    for copy in copies[5:]:
        copy.wait()


def prepare(rep, *arrays):
    vmem = pl.BlockSpec(memory_space=pltpu.VMEM)
    wide = 2 * HEAD_SIZE
    return pl.pallas_call(
        prepare_kernel,
        out_shape=(
            jax.ShapeDtypeStruct((Z, 2, HALF, HEAD_SIZE), bf16),
            jax.ShapeDtypeStruct((PACKED, wide), bf16),
        ),
        in_specs=[pl.BlockSpec(memory_space=pltpu.SMEM)] + [pl.BlockSpec(memory_space=pltpu.HBM)] * 7,
        out_specs=(vmem, vmem),
        scratch_shapes=[
            pltpu.VMEM((SLAB_QUERIES, wide), bf16),
            pltpu.VMEM((2, SLAB_QUERIES), f32),
            pltpu.VMEM((2, 4, CORES * Z * Y * X), jnp.int32),
            pltpu.SemaphoreType.DMA((5 + 4 * KEY_VALUE_HEADS,)),
        ],
        name="prepare",
    )(rep, *arrays)


def place_kernel(back, key_grad, value_grad):
    for g in range(KEY_VALUE_HEADS):
        for half in range(2):
            at = (slice(half * HALF, (half + 1) * HALF), slice(g * HEAD_SIZE, (g + 1) * HEAD_SIZE))
            key_grad[at] = back[2 * g + half, 0]
            value_grad[at] = back[2 * g + half, 1]


def placed(back):
    vmem = pl.BlockSpec(memory_space=pltpu.VMEM)
    return pl.pallas_call(
        place_kernel,
        out_shape=(jax.ShapeDtypeStruct((BLK, KEY_VALUE_HEADS * HEAD_SIZE), bf16),) * 2,
        in_specs=[vmem],
        out_specs=(vmem, vmem),
        compiler_params=pltpu.CompilerParams(vmem_limit_bytes=8 * 2**20),
        name="place",
    )(back)


def halve_kernel(bit, keep, got, own, sent):
    mine, other = bit[0], 1 - bit[0]
    for i in range(own.shape[0]):
        own[i] = keep[i, mine].astype(f32) + got[i, mine].astype(f32)
        sent[i] = (keep[i, other].astype(f32) + got[i, other].astype(f32)).astype(bf16)


def halve(bit, keep, got):
    count = keep.size // (2 * TILE * 2 * HEAD_SIZE)
    half = (count, TILE, 2 * HEAD_SIZE)
    whole = (count, 2, TILE, 2 * HEAD_SIZE)
    vmem = pl.BlockSpec(memory_space=pltpu.VMEM)
    return pl.pallas_call(
        halve_kernel,
        out_shape=(jax.ShapeDtypeStruct(half, f32), jax.ShapeDtypeStruct(half, bf16)),
        in_specs=[pl.BlockSpec(memory_space=pltpu.SMEM), vmem, vmem],
        out_specs=(vmem, vmem),
        compiler_params=pltpu.CompilerParams(vmem_limit_bytes=8 * 2**20),
        name="halve",
    )(jnp.full((1,), bit, jnp.int32), keep.reshape(whole), got.reshape(whole))


def across(value, axis, distance):
    return lax.ppermute(value, axis, [(i, i ^ distance) for i in range(4)])


def stage_kernel(x0, x1, x2, x3, qs, gs, qt, gt, norm, dots):
    for s, x in enumerate((x0, x1, x2, x3)):
        aux = x[2 * SLAB_QUERIES:].astype(f32)
        aux = aux[:8] + aux[8:16]
        for l in range(2):
            h, lanes = 2 * s + l, slice(l * HEAD_SIZE, (l + 1) * HEAD_SIZE)
            q, g = x[:SLAB_QUERIES, lanes], x[SLAB_QUERIES:2 * SLAB_QUERIES, lanes]
            qs[h], gs[h], qt[h], gt[h] = q, g, q.T, g.T
            dots[h] = jnp.concatenate([aux[2 * l:2 * l + 1], aux[2 * l + 1:2 * l + 2]], axis=1)
            norm[h] = jnp.concatenate([aux[2 * l + 4:2 * l + 5], aux[2 * l + 5:2 * l + 6]], axis=1)


def staged(xs):
    vmem = pl.BlockSpec(memory_space=pltpu.VMEM)
    heads = 2 * SLOTS
    return pl.pallas_call(
        stage_kernel,
        out_shape=(
            (jax.ShapeDtypeStruct((heads, SLAB_QUERIES, HEAD_SIZE), bf16),) * 2
            + (jax.ShapeDtypeStruct((heads, HEAD_SIZE, SLAB_QUERIES), bf16),) * 2
            + (jax.ShapeDtypeStruct((heads, 1, SLAB_QUERIES), f32),) * 2
        ),
        in_specs=[vmem] * SLOTS,
        out_specs=(vmem,) * 6,
        compiler_params=pltpu.CompilerParams(vmem_limit_bytes=16 * 2**20),
        name="stage",
    )(*xs)


def attention_kernel(mask, order, kv, q_in, g_in, qt_in, gt_in, norm, dots, dkv, keep, send,
                     qs, gs, qt, gt, kbuf, vbuf, dk, dv, dq, sems):
    scale = HEAD_SIZE ** -0.5

    def fetches(h):
        pairs = ((qt_in, qt), (gt_in, gt), (g_in, gs), (q_in, qs))
        return [
            pltpu.make_async_copy(source.at[h], target.at[h], sems.at[h, i])
            for i, (source, target) in enumerate(pairs)
        ]

    for h in range(2 * SLOTS):
        for copy in fetches(h):
            copy.start()
    dk[...] = jnp.zeros_like(dk)
    dv[...] = jnp.zeros_like(dv)
    dq[...] = jnp.zeros_like(dq)

    def head(h, _):
        for copy in fetches(h):
            copy.wait()

        def turn(t, _):
            picked = [order[h, t * PICK + j] for j in range(PICK)]
            rows = []
            for j, i in enumerate(picked):
                kbuf[pl.ds(j * HALF, HALF), :] = kv[i, 0]
                vbuf[pl.ds(j * HALF, HALF), :] = kv[i, 1]
                row = jnp.concatenate(
                    [
                        jnp.where(mask[h * 4 + qb, i] > 0, norm[h, :, pl.ds(qb * BLK, BLK)], NEVER)
                        for qb in range(4)
                    ],
                    axis=1,
                )
                rows.append(jnp.broadcast_to(row, (HALF, SLAB_QUERIES)))
            bias = jnp.concatenate(rows, axis=0)
            q, g = qs[h], gs[h]
            scores = dot(kbuf[...], qt[h], ((1,), (0,)))
            w = jnp.exp2(scores * (scale * LOG2E) + bias)
            gw = dot(vbuf[...], gt[h], ((1,), (0,)))
            ds = (w * (gw - dots[h])).astype(bf16)
            dv_part = dot(w.astype(bf16), g, ((1,), (0,)))
            dk_part = dot(ds, q, ((1,), (0,)))
            for j, i in enumerate(picked):
                dv[i] += dv_part[j * HALF:(j + 1) * HALF]
                dk[i] += dk_part[j * HALF:(j + 1) * HALF]
            dq[h] += dot(kbuf[...], ds, ((0,), (0,)))
            return 0

        lax.fori_loop(0, order[h, Z], turn, 0)
        return 0

    lax.fori_loop(0, 2 * SLOTS, head, 0)
    dkv[:, 0] = (dk[...] * scale).astype(bf16)
    dkv[:, 1] = dv[...].astype(bf16)
    for s in range(SLOTS):
        for l in range(2):
            lanes = pl.ds(l * HEAD_SIZE, HEAD_SIZE)
            part = (dq[2 * s + l] * scale).astype(bf16).T
            if s % 2 == 0:
                keep[s // 2, :, lanes] = part
            else:
                send[s // 2, :, lanes] = part


def attention(mask, order, kv, xs):
    vmem = pl.BlockSpec(memory_space=pltpu.VMEM)
    rows = (SLAB_QUERIES, 2 * HEAD_SIZE)
    return pl.pallas_call(
        attention_kernel,
        out_shape=(
            jax.ShapeDtypeStruct((Z, 2, HALF, HEAD_SIZE), bf16),
            jax.ShapeDtypeStruct((2, *rows), bf16),
            jax.ShapeDtypeStruct((2, *rows), bf16),
        ),
        in_specs=[pl.BlockSpec(memory_space=pltpu.SMEM)] * 2 + [vmem] + [pl.BlockSpec(memory_space=pl.ANY)] * 4 + [vmem] * 2,
        out_specs=(vmem, vmem, vmem),
        scratch_shapes=[
            pltpu.VMEM((2 * SLOTS, SLAB_QUERIES, HEAD_SIZE), bf16),
            pltpu.VMEM((2 * SLOTS, SLAB_QUERIES, HEAD_SIZE), bf16),
            pltpu.VMEM((2 * SLOTS, HEAD_SIZE, SLAB_QUERIES), bf16),
            pltpu.VMEM((2 * SLOTS, HEAD_SIZE, SLAB_QUERIES), bf16),
            pltpu.VMEM((PICK * HALF, HEAD_SIZE), bf16),
            pltpu.VMEM((PICK * HALF, HEAD_SIZE), bf16),
            pltpu.VMEM((Z, HALF, HEAD_SIZE), f32),
            pltpu.VMEM((Z, HALF, HEAD_SIZE), f32),
            pltpu.VMEM((2 * SLOTS, HEAD_SIZE, SLAB_QUERIES), f32),
            pltpu.SemaphoreType.DMA((2 * SLOTS, 4)),
        ],
        compiler_params=pltpu.CompilerParams(vmem_limit_bytes=51 * 2**20),
        cost_estimate=pl.CostEstimate(
            flops=5 * 2 * 4096 * 1024 * 128 // 3,
            bytes_accessed=6 * 2**20,
            transcendentals=4096 * 1024 // 3,
        ),
        name="attention",
    )(mask, order, kv, *xs)


def attended_first(mask):
    live = jnp.max(mask.reshape(2 * SLOTS, 4, Z), axis=1)
    index = jnp.arange(Z)
    earlier = (index[:, None] < index[None, :]).astype(jnp.int32)
    before = jnp.sum(live[:, :, None] * earlier, axis=1)
    count = jnp.sum(live, axis=1, keepdims=True)
    rank = jnp.where(live > 0, before, count + index[None, :] - before)
    order = jnp.sum(jnp.where(rank[:, :, None] == index, index[None, :, None], 0), axis=1)
    return jnp.concatenate([order, (count + PICK - 1) // PICK], axis=1).astype(jnp.int32)


def other_core(value):
    return lax.ppermute(value, "core", [(0, 1), (1, 0)])


def other_chip(value):
    return lax.ppermute(value, "z", [(z, z ^ 1) for z in range(Z)])


def compute(queries, keys, values, forward_output, output_gradient, log_sum_norm, block_attend_mask):
    core, y, x = (lax.axis_index(axis) for axis in ("core", "y", "x"))
    own_kv, x0 = prepare(
        jnp.full((1,), y * X + x, jnp.int32), queries, keys, values, forward_output, output_gradient,
        log_sum_norm, block_attend_mask,
    )
    x2 = other_chip(x0)
    kv = lax.all_to_all(own_kv, "z", 0, 0, tiled=True)
    x1 = other_core(x0)
    x3 = other_core(x2)
    slots = (x0, x1, x2, x3)
    at = 2 * SLAB_QUERIES + 16
    operands = staged(slots)
    attended = [a[at:at + 8] for a in slots[:3]]
    attended.append(other_core(attended[2]))
    mask = jnp.concatenate(
        [lax.dynamic_slice_in_dim(a, core * Z, Z, 1) for a in attended]
    ).astype(jnp.int32)

    dkv, keep, send = attention(mask, attended_first(mask), kv, operands)

    got = other_core(send)
    own, sent = halve(x % 2, keep, got)
    got = across(sent, "x", 1)
    back = lax.all_to_all(dkv, "z", 0, 0, tiled=True)
    for bit, axis, distance in ((x // 2, "x", 2), (y % 2, "y", 1), (y // 2, "y", 2)):
        own, sent = halve(bit, own, got)
        got = across(sent, axis, distance)
    total = own + got.astype(f32)
    other = other_chip(total[1].astype(bf16))
    grad_queries = (total[0] + other.astype(f32)).astype(bf16)
    key_grad, value_grad = placed(back)
    return grad_queries, key_grad, value_grad


def solution(mesh):
    fine = Mesh(mesh.devices.reshape(Z, CORES, Y, X), ("z", "core", "y", "x"))
    ctx, rep = ("z", "core"), ("y", "x")
    in_specs = (
        P(None, ctx),
        P((*ctx, *rep), None),
        P((*ctx, *rep), None),
        P(None, ctx),
        P(None, ctx),
        P(ctx, None),
        P(ctx, None, None),
    )
    out_specs = (P(rep, ctx), P((*ctx, *rep), None), P((*ctx, *rep), None))
    return jax.shard_map(compute, mesh=fine, in_specs=in_specs, out_specs=out_specs, check_vma=False)
```
